256 devices in a mesh: seq: 64 (over y, z, core), head: 4 (over x).
Axes of the slice: x: 4, y: 4, z: 8, core: 2. Of those that a mesh axis runs over, the one named last changes fastest.
Arguments:
- tokens: bfloat16 [16384, 2048], P('seq')
- w_qkv: bfloat16 [2048, 3, 2048], P(None, None, 'head'), may hold values from -0.125 to 0.125
- w_out: bfloat16 [2048, 2048], P('head'), may hold values from -0.125 to 0.125
- norm_gain: float32 [2048], replicated, may hold values from 0.25 to 1.75
- w_label: bfloat16 [2048, 128], replicated, may hold values from -0.125 to 0.125
- offset_mid: int32 [16], P('head'), may hold values from 0 to 7
- offset_far: int32 [16], P('head'), may hold values from 0 to 63
Outputs:
- logits: float32 [16384, 128], P('seq')
The draws below stay inside these ranges and needn't reach their ends.
All inputs are finite; a program needn't handle non-finite values.
Results may differ from the reference program's by a relative error of at most 0.023.
The reference program's roundings to bfloat16 on the way (of `qkv`, `attn` and `scaled`) count: a program that leaves them out, or rounds other values in their place, can miss the bound.
Values may be sent and summed in bfloat16 or wider, within the bound.
No kernel may reach another device: no remote copies, remote signals or barrier semaphores. Data moves between devices by JAX's collectives and lax.ppermute only.
A program may use at most 64 MiB of HBM per device.

```python
import jax
import jax.numpy as jnp
from jax import lax

D = 2048
HEADS = 16
HEAD_DIM = 128
CLASSES = 128
SPAN = 8
TOK_DEV = 256
TOKENS = 16384
N_SEQ = 64
N_HEAD = 4


def draw_tokens(key, part):
    base = jax.random.normal(jax.random.fold_in(key, 11), (TOKENS, D), jnp.float32)
    base = jnp.clip(base, -6.0, 6.0) * 4.0
    return base.astype(jnp.bfloat16)


def place_ends(values, key, least, largest):
    longest = values.shape.index(max(values.shape))
    spots = []
    for shift in (0, 1):
        where = [jax.random.randint(jax.random.fold_in(key, axis), (), 0, length) for axis, length in enumerate(values.shape)]
        where[longest] = (where[longest] + shift) % values.shape[longest]
        spots.append(tuple(where))
    return values.at[spots[0]].set(least).at[spots[1]].set(largest)


def block_levels(own_key, shape, shards, least, top_value):
    def one(dim, shards_of):
        draws = jax.random.uniform(jax.random.fold_in(jax.random.fold_in(own_key, 6), dim), (shards_of,), jnp.float32, least / len(shards), top_value / len(shards))
        return jnp.repeat(jnp.exp(draws), shape[dim] // shards_of).reshape((-1,) + (1,) * (len(shape) - dim - 1))

    loudness = one(*shards[0])
    for cut in shards[1:]:
        loudness = loudness * one(*cut)
    return loudness


def scatter_about(key, shape, scale, bound, split=(), kind=jnp.bfloat16):
    result = jax.random.normal(key, shape, jnp.float32) * scale
    if len(split) > 0:
        result = block_levels(key, shape, split, -0.22, 0.18) * result
    return jnp.clip(result, min=-bound, max=bound).astype(kind)


def setup_inputs(seed: int = 0) -> dict:
    key_of = jax.random.split(jax.random.key(seed), 8)
    tokens = draw_tokens(jax.random.fold_in(key_of[7], 71), 0)
    w_qkv = scatter_about(key_of[1], (D, 3, D), D ** -0.5, 0.125, ((2, 4),))
    w_out = scatter_about(key_of[2], (D, D), D ** -0.5, 0.125, ((0, 4),))
    norm_gain = jnp.clip(1.0 + 0.15 * jax.random.normal(key_of[3], (D,), jnp.float32), 0.25, 1.75)
    w_label = scatter_about(key_of[4], (D, CLASSES), D ** -0.5, 0.125)
    offset_mid = place_ends(jax.random.randint(key_of[5], (HEADS,), 0, SPAN), jax.random.fold_in(key_of[5], 1), 0, SPAN - 1).astype(jnp.int32)
    offset_far = place_ends(jax.random.randint(key_of[6], (HEADS,), 0, N_SEQ), jax.random.fold_in(key_of[6], 1), 0, N_SEQ - 1).astype(jnp.int32)
    return {"tokens": tokens, "w_qkv": w_qkv, "w_out": w_out, "norm_gain": norm_gain, "w_label": w_label, "offset_mid": offset_mid, "offset_far": offset_far}


def attend(queries, keys, values):
    scores = jnp.einsum('rhe,she->hrs', queries.astype(jnp.float32), keys.astype(jnp.float32)) / jnp.sqrt(jnp.float32(HEAD_DIM))
    top = lax.optimization_barrier(jnp.max(scores, axis=-1))
    weights = jnp.exp(scores - top[..., None])
    total = lax.optimization_barrier(jnp.sum(weights, axis=-1))
    weights = weights.astype(jnp.bfloat16).astype(jnp.float32)
    summed = jnp.einsum('hrs,she->rhe', weights, values.astype(jnp.float32))
    return (top.T, total.T, summed)

def select_rows(array, offsets, rate):
    rows = array.shape[0] // rate
    shaped = array.reshape(rows, rate, array.shape[1], array.shape[2])
    index = jnp.broadcast_to(offsets.astype(jnp.int32)[None, None, :, None], (rows, 1, array.shape[1], array.shape[2]))
    return jnp.take_along_axis(shaped, index, axis=1)[:, 0]

def spread_rows(parts, offsets, rate):
    top, total, summed = parts
    rows = top.shape[0]
    marks = jnp.arange(rate, dtype=jnp.int32)[None, :, None] == offsets.astype(jnp.int32)[None, None, :]
    top_full = jnp.where(marks, top[:, None, :], jnp.float32(-1e+30)).reshape(rows * rate, -1)
    total_full = jnp.where(marks, total[:, None, :], jnp.float32(0.0)).reshape(rows * rate, -1)
    sum_full = jnp.where(marks[..., None], summed[:, None], jnp.float32(0.0)).reshape(rows * rate, summed.shape[1], summed.shape[2])
    return (top_full, total_full, sum_full)

def branch(queries, keys, values, offsets, rate, segment, turn):
    sel_q = select_rows(queries, offsets, rate)
    sel_k = select_rows(keys, offsets, rate)
    sel_v = select_rows(values, offsets, rate)
    if turn:
        sel_q = jnp.roll(sel_q, turn, axis=0)
        sel_k = jnp.roll(sel_k, turn, axis=0)
        sel_v = jnp.roll(sel_v, turn, axis=0)
    groups = sel_q.shape[0] // segment
    shaped = lambda a: a.reshape(groups, segment, a.shape[1], a.shape[2])
    top, total, summed = lax.map(lambda t: attend(t[0], t[1], t[2]), (shaped(sel_q), shaped(sel_k), shaped(sel_v)))
    top = top.reshape(-1, HEADS)
    total = total.reshape(-1, HEADS)
    summed = summed.reshape(-1, HEADS, HEAD_DIM)
    if turn:
        top = jnp.roll(top, -turn, axis=0)
        total = jnp.roll(total, -turn, axis=0)
        summed = jnp.roll(summed, -turn, axis=0)
    return spread_rows((top, total, summed), offsets, rate)

def reference(tokens, w_qkv, w_out, norm_gain, w_label, offset_mid, offset_far):
    qkv = jnp.dot(tokens, w_qkv.reshape(D, 3 * D), preferred_element_type=jnp.float32).astype(jnp.bfloat16)
    qkv = qkv.reshape(TOKENS, 3, HEADS, HEAD_DIM)
    queries, keys, values = (qkv[:, 0], qkv[:, 1], qkv[:, 2])
    zeros = jnp.zeros((HEADS,), jnp.int32)
    middle_turn = SPAN // 2 * (TOK_DEV // SPAN)
    branches = [branch(queries, keys, values, zeros, 1, TOK_DEV, 0), branch(queries, keys, values, offset_mid, SPAN, TOK_DEV, middle_turn), branch(queries, keys, values, offset_far, N_SEQ, TOK_DEV, 0)]
    peak = jnp.maximum(jnp.maximum(branches[0][0], branches[1][0]), branches[2][0])
    upper = jnp.zeros((TOKENS, HEADS, HEAD_DIM), jnp.float32)
    lower = jnp.zeros((TOKENS, HEADS), jnp.float32)
    for top, total, summed in branches:
        factor = jnp.exp(top - peak)
        upper = upper + factor[..., None] * summed
        lower = lower + factor * total
    attn = (upper / lower[..., None]).astype(jnp.bfloat16).reshape(TOKENS, D)
    group = D // N_HEAD
    mixed = tokens.astype(jnp.float32)
    for index in range(N_HEAD):
        part = jnp.dot(attn[:, index * group:(index + 1) * group], w_out[index * group:(index + 1) * group], preferred_element_type=jnp.float32)
        mixed = mixed + part.astype(jnp.bfloat16).astype(jnp.float32)
    mean_sq = lax.optimization_barrier(jnp.mean(mixed * mixed, axis=-1))
    scaled = (mixed * norm_gain).astype(jnp.bfloat16)
    product = jnp.dot(scaled, w_label, preferred_element_type=jnp.float32)
    return product / jnp.sqrt(mean_sq + 1e-05)[:, None]
```

```python
import jax
import jax.numpy as jnp
from jax import lax
from jax.sharding import PartitionSpec as P

SPAN = 8


def segments(seq_count):
    return [
        [(SPAN * k - SPAN // 2 + i) % seq_count for i in range(SPAN)]
        for k in range(seq_count // SPAN)
    ]


def share(block, axis, groups):
    pieces = [block]
    for step in range(1, len(groups[0])):
        route = [(g[i], g[i ^ step]) for g in groups for i in range(len(g))]
        pieces.append(lax.ppermute(block, axis, route))
    return jnp.stack(pieces)


def attend(queries, keys, values):
    scores = jnp.einsum(
        "hre,hse->hrs", queries, keys, preferred_element_type=jnp.float32
    ) / jnp.sqrt(jnp.float32(queries.shape[2]))
    top = jnp.max(scores, axis=-1, keepdims=True)
    weights = jnp.exp(scores - top)
    total = jnp.sum(weights, axis=-1, keepdims=True)
    summed = jnp.einsum(
        "hrs,hse->hre", weights.astype(jnp.bfloat16), values, preferred_element_type=jnp.float32
    )
    return (top, total, summed)


def pick(offsets, rows, rate):
    where = jnp.arange(rows // rate, dtype=jnp.int32)[None, :, None] * rate
    where = where + offsets[:, None, None]
    return where == jnp.arange(rows, dtype=jnp.int32)[None, None, :]


def take(marks, array):
    return jnp.einsum(
        "hjr,hre->hje",
        marks.astype(jnp.bfloat16),
        array,
        preferred_element_type=jnp.float32,
    ).astype(jnp.bfloat16)


def spread(marks, parts):
    top, total, summed = parts
    hit = jnp.any(marks, axis=1)[..., None]
    put = lambda a: jnp.einsum(
        "hjr,hje->hre", marks.astype(jnp.float32), a, precision=lax.Precision.HIGHEST
    )
    return (jnp.where(hit, put(top), jnp.float32(-1e30)), put(total), put(summed))


def body(tokens, w_qkv, w_out, norm_gain, w_label, offset_mid, offset_far):
    tok_rows, width = tokens.shape
    local_heads = offset_mid.shape[0]
    head_size = w_qkv.shape[2] // local_heads
    seq_count = lax.axis_size("seq")
    head_count = lax.axis_size("head")
    split = lambda a: a.reshape(tok_rows, local_heads, head_size).transpose(1, 0, 2)
    qkv = [
        split(
            jnp.dot(tokens, w_qkv[:, c], preferred_element_type=jnp.float32).astype(jnp.bfloat16)
        )
        for c in range(3)
    ]
    queries, keys, values = qkv

    groups = segments(seq_count)
    across = [[g[2 * i + c] for i in range(SPAN // 2)] for g in groups for c in range(2)]
    cores = [[2 * i, 2 * i + 1] for i in range(seq_count // 2)]
    along_z = [[16 * y + 2 * z + c for z in range(8)] for y in range(4) for c in range(2)]
    along_y = [[16 * y + r for y in range(4)] for r in range(16)]

    mid_marks = pick(offset_mid, tok_rows, SPAN)
    far_marks = pick(offset_far, tok_rows, seq_count)
    mid_kv = jnp.stack([take(mid_marks, keys), take(mid_marks, values)])
    far_kv = jnp.stack([take(far_marks, keys), take(far_marks, values)])
    mid_all = share(share(mid_kv, "seq", across), "seq", cores)
    far_all = share(share(share(far_kv, "seq", along_z), "seq", along_y), "seq", cores)
    gather = lambda a: jnp.moveaxis(
        a.reshape((-1,) + a.shape[-4:]), 0, 2
    ).reshape(2, local_heads, -1, head_size)
    mid_all = gather(mid_all)
    far_all = gather(far_all)

    near = attend(queries, keys, values)
    middle = spread(mid_marks, attend(take(mid_marks, queries), mid_all[0], mid_all[1]))
    distant = spread(far_marks, attend(take(far_marks, queries), far_all[0], far_all[1]))
    branches = [near, middle, distant]
    peak = jnp.maximum(jnp.maximum(near[0], middle[0]), distant[0])
    upper = sum(jnp.exp(top - peak) * summed for top, total, summed in branches)
    lower = sum(jnp.exp(top - peak) * total for top, total, summed in branches)
    attn = (upper / lower).astype(jnp.bfloat16)
    attn = attn.transpose(1, 0, 2).reshape(tok_rows, local_heads * head_size)
    part = jnp.dot(attn, w_out, preferred_element_type=jnp.float32).astype(jnp.bfloat16)

    place = lax.axis_index("head")
    own_rows = tok_rows // head_count
    quarter = lambda a, i: lax.dynamic_slice_in_dim(a, i * own_rows, own_rows, 0)
    mixed = quarter(tokens, place).astype(jnp.float32) + quarter(part, place).astype(jnp.float32)
    for step in range(1, head_count):
        route = [(i, i ^ step) for i in range(head_count)]
        mixed = mixed + lax.ppermute(quarter(part, place ^ step), "head", route).astype(
            jnp.float32
        )
    mean_sq = jnp.mean(mixed * mixed, axis=-1)
    scaled = (mixed * norm_gain).astype(jnp.bfloat16)
    product = jnp.dot(scaled, w_label, preferred_element_type=jnp.float32)
    own = product / jnp.sqrt(mean_sq + 1e-05)[:, None]
    logits = jnp.zeros((head_count,) + own.shape, jnp.float32)
    every = share(own, "head", [list(range(head_count))])
    for step in range(head_count):
        logits = lax.dynamic_update_index_in_dim(logits, every[step], place ^ step, 0)
    return logits.reshape(tok_rows, -1)


def solution(mesh):
    return jax.shard_map(
        body,
        mesh=mesh,
        in_specs=(
            P("seq", None),
            P(None, None, "head"),
            P("head", None),
            P(),
            P(),
            P("head"),
            P("head"),
        ),
        out_specs=P("seq", None),
        check_vma=False,
    )
```

```python
import functools

import jax
import jax.numpy as jnp
from jax import lax
from jax.experimental import pallas as pl
from jax.experimental.pallas import tpu as pltpu
from jax.sharding import PartitionSpec as P

SPAN = 8
PICKS = 40
LOW = -1e30
VMEM = pl.BlockSpec(memory_space=pltpu.VMEM)
SMEM = pl.BlockSpec(memory_space=pltpu.SMEM)
PARAMS = pltpu.CompilerParams(vmem_limit_bytes=48 << 20)


def segments(seq_count):
    return [
        [(SPAN * k - SPAN // 2 + i) % seq_count for i in range(SPAN)]
        for k in range(seq_count // SPAN)
    ]


def share(block, axis, groups):
    pieces = [block]
    for step in range(1, len(groups[0])):
        route = [(g[i], g[i ^ step]) for g in groups for i in range(len(g))]
        pieces.append(lax.ppermute(block, axis, route))
    return pieces


def dot(a, b):
    return jnp.dot(a, b, preferred_element_type=jnp.float32)


def dot_t(a, b):
    return lax.dot_general(a, b, (((1,), (1,)), ((), ())), preferred_element_type=jnp.float32)


def picked_rows(c, mid, far, mid_rows, seq_count):
    last = (c >= mid_rows) & (c < mid_rows + 4)
    other = jnp.where(last, (c - mid_rows) * seq_count + far, -1)
    return jnp.where(c < mid_rows, c * SPAN + mid, other)


def kv_kernel(rows, heads, size, seq_count, mid_ref, far_ref, tok_ref, w_ref,
              kv_ref, mid_out, far_out, acc_ref, few_ref):
    step = pl.program_id(1)
    part = dot(tok_ref[...], w_ref[...])

    @pl.when(step == 0)
    def _():
        acc_ref[...] = part

    @pl.when(step > 0)
    def _():
        acc_ref[...] += part

    @pl.when(step == pl.num_programs(1) - 1)
    def _():
        whole = acc_ref[...].astype(jnp.bfloat16)
        kv_ref[...] = whole
        mid_rows = rows // SPAN
        c = lax.broadcasted_iota(jnp.int32, (PICKS, rows), 0)
        r = lax.broadcasted_iota(jnp.int32, (PICKS, rows), 1)
        for h in range(heads):
            target = picked_rows(c, mid_ref[h], far_ref[h], mid_rows, seq_count)
            marks = jnp.where(r == target, 1.0, 0.0).astype(jnp.bfloat16)
            got = dot(marks, whole[:, h * size : (h + 1) * size])
            mid_out[h] = got[:mid_rows].astype(jnp.bfloat16)
            few_ref[pl.ds(4 * h, 4)] = got[mid_rows : mid_rows + 4]
        far_out[...] = few_ref[...].astype(jnp.bfloat16)


def near_kernel(rows, heads, size, seq_count, mid_ref, far_ref, tok_ref, w_ref, kv_ref,
                near_ref, sel_ref, acc_ref):
    step = pl.program_id(0)
    part = dot(tok_ref[...], w_ref[...])

    @pl.when(step == 0)
    def _():
        acc_ref[...] = part

    @pl.when(step > 0)
    def _():
        acc_ref[...] += part

    @pl.when(step == pl.num_programs(0) - 1)
    def _():
        whole = acc_ref[...].astype(jnp.bfloat16)
        mid_rows = rows // SPAN
        c = lax.broadcasted_iota(jnp.int32, (PICKS, rows), 0)
        r = lax.broadcasted_iota(jnp.int32, (PICKS, rows), 1)
        for h in range(heads):
            cols = slice(h * size, (h + 1) * size)
            queries = whole[:, cols]
            target = picked_rows(c, mid_ref[h], far_ref[h], mid_rows, seq_count)
            marks = jnp.where(r == target, 1.0, 0.0).astype(jnp.bfloat16)
            sel_ref[h] = dot(marks, queries).astype(jnp.bfloat16)
            scores = dot_t(queries, kv_ref[0, :, cols]) * size**-0.5
            top = jnp.max(scores, axis=1, keepdims=True)
            weights = jnp.exp(scores - top)
            total = jnp.sum(weights, axis=1, keepdims=True)
            summed = dot(weights.astype(jnp.bfloat16), kv_ref[1, :, cols])
            near_ref[:, cols] = (summed / total).astype(jnp.bfloat16)


def softmax_parts(scores, values):
    top = jnp.max(scores, axis=1, keepdims=True)
    weights = jnp.exp(scores - top)
    total = jnp.sum(weights, axis=1, keepdims=True)
    return top, total, dot(weights.astype(jnp.bfloat16), values)


def wide_kernel(rows, heads, size, seq_count, quarters,
                mid_ref, far_ref, place_ref, sel_ref, kv_ref, near_ref, *refs):
    mid_pieces, mid_other, far_pieces, far_other, w_ref = (
        refs[0:4], refs[4], refs[5:9], refs[9], refs[10]
    )
    outs, attn_ref = refs[11 : 11 + quarters], refs[11 + quarters]
    mid_rows = rows // SPAN
    scale = size**-0.5
    far_rows = lambda i: jnp.concatenate(
        [ref[:, i].reshape(-1, size) for ref in far_pieces]
        + [far_other[j, :, i].reshape(-1, size) for j in range(4)]
    )
    far_q = jnp.concatenate([sel_ref[h].astype(jnp.float32)[mid_rows:] for h in range(heads)])
    far_scores = dot_t(far_q.astype(jnp.bfloat16), far_rows(0)) * scale
    q_head = lax.broadcasted_iota(jnp.int32, far_scores.shape, 0) // 8
    k_head = (lax.broadcasted_iota(jnp.int32, far_scores.shape, 1) % 16) // 4
    far_top, far_total, far_sum = softmax_parts(
        jnp.where(q_head == k_head, far_scores, LOW), far_rows(1)
    )
    for h in range(heads):
        cols = slice(h * size, (h + 1) * size)
        mid_off, far_off = mid_ref[h], far_ref[h]
        stack = lambda i: jnp.concatenate(
            [kv_ref[i, :, cols]]
            + [ref[i, h] for ref in mid_pieces]
            + [mid_other[j, i, h] for j in range(4)]
        )
        scores = dot_t(sel_ref[h], stack(0)) * scale
        row = lax.broadcasted_iota(jnp.int32, scores.shape, 0)
        col = lax.broadcasted_iota(jnp.int32, scores.shape, 1)
        both = ((far_off + SPAN - mid_off) & (SPAN - 1)) == 0
        keep = (row < mid_rows) | (col < rows) | both
        top, total, summed = softmax_parts(jnp.where(keep, scores, LOW), stack(1))
        attn = summed / total
        far = slice(8 * h, 8 * h + 8)
        peak = jnp.maximum(top[mid_rows:], far_top[far])
        mine = jnp.exp(top[mid_rows:] - peak)
        other = jnp.exp(far_top[far] - peak)
        attn_far = (mine * summed[mid_rows:] + other * far_sum[far]) / (
            mine * total[mid_rows:] + other * far_total[far]
        )
        attn = jnp.concatenate([attn[:mid_rows], attn_far]).astype(jnp.bfloat16)
        r = lax.broadcasted_iota(jnp.int32, (rows, PICKS), 0)
        c = lax.broadcasted_iota(jnp.int32, (rows, PICKS), 1)
        target = picked_rows(c, mid_off, far_off, mid_rows, seq_count)
        twice = (c < mid_rows) & (
            ((target + seq_count - far_off) & (seq_count - 1)) == 0
        )
        marks = jnp.where((r == target) & jnp.logical_not(twice), 1.0, 0.0)
        hit = jnp.sum(marks, axis=1, keepdims=True) > 0.5
        put = dot(marks.astype(jnp.bfloat16), attn)
        attn_ref[:, cols] = jnp.where(hit, put, near_ref[:, cols].astype(jnp.float32))
    own = rows // quarters
    place = place_ref[0]
    order = jnp.concatenate(
        [
            attn_ref[pl.ds(pl.multiple_of((place ^ s) * own, own), own), :]
            for s in range(quarters)
        ]
    ).astype(jnp.bfloat16)
    chunk = 512
    for start in range(0, w_ref.shape[1], chunk):
        part = dot(order, w_ref[:, start : start + chunk]).astype(jnp.bfloat16)
        for s in range(quarters):
            outs[s][:, start : start + chunk] = part[s * own : (s + 1) * own]


def logits_kernel(place_ref, tok_ref, gain_ref, label_ref, *refs):
    out_ref = refs[-1]
    mixed = tok_ref[...].astype(jnp.float32)
    for ref in refs[:-1]:
        mixed = mixed + ref[...].astype(jnp.float32)
    mean_sq = jnp.mean(mixed * mixed, axis=1, keepdims=True)
    scaled = (mixed * gain_ref[...]).astype(jnp.bfloat16)
    out_ref[...] = dot(scaled, label_ref[...]) / jnp.sqrt(mean_sq + 1e-05)


def body(tokens, w_qkv, w_out, norm_gain, w_label, offset_mid, offset_far):
    rows, width = tokens.shape
    heads = offset_mid.shape[0]
    cols = w_qkv.shape[2]
    size = cols // heads
    seq_count = lax.axis_size("seq")
    head_count = lax.axis_size("head")
    place = lax.axis_index("head")
    mid_rows = rows // SPAN
    sizes = (rows, heads, size, seq_count)
    bf16 = lambda *shape: jax.ShapeDtypeStruct(shape, jnp.bfloat16)
    weights = w_qkv.transpose(1, 0, 2)
    deep = 512

    kv, mid_kv, far_kv = pl.pallas_call(
        functools.partial(kv_kernel, *sizes),
        grid=(2, width // deep),
        in_specs=[
            SMEM,
            SMEM,
            pl.BlockSpec((rows, deep), lambda c, k: (0, k)),
            pl.BlockSpec((None, deep, cols), lambda c, k: (1 + c, k, 0)),
        ],
        out_specs=[
            pl.BlockSpec((None, rows, cols), lambda c, k: (c, 0, 0)),
            pl.BlockSpec((None, heads, mid_rows, size), lambda c, k: (c, 0, 0, 0)),
            pl.BlockSpec((None, 4 * heads, size), lambda c, k: (c, 0, 0)),
        ],
        out_shape=[bf16(2, rows, cols), bf16(2, heads, mid_rows, size), bf16(2, 4 * heads, size)],
        scratch_shapes=[
            pltpu.VMEM((rows, cols), jnp.float32),
            pltpu.VMEM((4 * heads, size), jnp.float32),
        ],
        compiler_params=PARAMS,
        name="keys_values",
    )(offset_mid, offset_far, tokens, weights)

    groups = segments(seq_count)
    across = [[g[2 * i + c] for i in range(SPAN // 2)] for g in groups for c in range(2)]
    cores = [(i, i ^ 1) for i in range(seq_count)]
    along_z = [[16 * y + 2 * z + c for z in range(8)] for y in range(4) for c in range(2)]
    along_y = [[16 * y + r for y in range(4)] for r in range(16)]
    mid_pieces = share(mid_kv, "seq", across)
    mid_other = lax.ppermute(jnp.stack(mid_pieces), "seq", cores)
    far_line = lax.all_to_all(
        jnp.broadcast_to(far_kv[None], (8,) + far_kv.shape), "seq", 0, 0, axis_index_groups=along_z
    )
    far_pieces = share(far_line, "seq", along_y)
    far_other = lax.ppermute(jnp.stack(far_pieces), "seq", cores)

    near, sel = pl.pallas_call(
        functools.partial(near_kernel, *sizes),
        grid=(width // deep,),
        in_specs=[
            SMEM,
            SMEM,
            pl.BlockSpec((rows, deep), lambda k: (0, k)),
            pl.BlockSpec((None, deep, cols), lambda k: (0, k, 0)),
            pl.BlockSpec((2, rows, cols), lambda k: (0, 0, 0)),
        ],
        out_specs=[
            pl.BlockSpec((rows, cols), lambda k: (0, 0)),
            pl.BlockSpec((heads, PICKS, size), lambda k: (0, 0, 0)),
        ],
        out_shape=[bf16(rows, cols), bf16(heads, PICKS, size)],
        scratch_shapes=[pltpu.VMEM((rows, cols), jnp.float32)],
        compiler_params=PARAMS,
        name="near",
    )(offset_mid, offset_far, tokens, weights, kv)

    own = rows // head_count
    place_arr = place.astype(jnp.int32).reshape(1)
    parts = pl.pallas_call(
        functools.partial(wide_kernel, *sizes, head_count),
        in_specs=[SMEM] * 3 + [VMEM] * 14,
        out_specs=[VMEM] * head_count,
        out_shape=[bf16(own, width)] * head_count,
        scratch_shapes=[pltpu.VMEM((rows, cols), jnp.float32)],
        compiler_params=PARAMS,
        name="wide",
    )(
        offset_mid, offset_far, place_arr, sel, kv, near,
        *mid_pieces, mid_other, *far_pieces, far_other, w_out,
    )

    got = [parts[0]]
    for step in range(1, head_count):
        route = [(i, i ^ step) for i in range(head_count)]
        got.append(lax.ppermute(parts[step], "head", route))

    whole = lambda *shape: pl.BlockSpec(shape, lambda i, p: (0,) * len(shape))
    logit = pl.pallas_call(
        logits_kernel,
        grid_spec=pltpu.PrefetchScalarGridSpec(
            num_scalar_prefetch=1,
            grid=(1,),
            in_specs=[
                pl.BlockSpec((own, width), lambda i, p: (p[0], 0)),
                whole(1, width),
                whole(*w_label.shape),
            ]
            + [whole(own, width)] * head_count,
            out_specs=whole(own, w_label.shape[1]),
        ),
        out_shape=jax.ShapeDtypeStruct((own, w_label.shape[1]), jnp.float32),
        compiler_params=PARAMS,
        name="logits",
    )(place_arr, tokens, norm_gain.reshape(1, width), w_label, *got)

    every = share(logit, "head", [list(range(head_count))])
    logits = jnp.zeros((head_count,) + logit.shape, jnp.float32)
    for step in range(head_count):
        logits = lax.dynamic_update_index_in_dim(logits, every[step], place ^ step, 0)
    return logits.reshape(rows, -1)


def solution(mesh):
    return jax.shard_map(
        body,
        mesh=mesh,
        in_specs=(
            P("seq", None),
            P(None, None, "head"),
            P("head", None),
            P(),
            P(),
            P("head"),
            P("head"),
        ),
        out_specs=P("seq", None),
        check_vma=False,
    )
```

```python
import functools

import jax
import jax.numpy as jnp
from jax import lax
from jax.experimental import pallas as pl
from jax.experimental.pallas import tpu as pltpu
from jax.sharding import PartitionSpec as P

SPAN = 8
PICKS = 40
LOW = -1e30
VMEM = pl.BlockSpec(memory_space=pltpu.VMEM)
HBM = pl.BlockSpec(memory_space=pltpu.HBM)
SMEM = pl.BlockSpec(memory_space=pltpu.SMEM)


def params(mib):
    return pltpu.CompilerParams(vmem_limit_bytes=mib << 20)


def segments(seq_count):
    return [
        [(SPAN * k - SPAN // 2 + i) % seq_count for i in range(SPAN)]
        for k in range(seq_count // SPAN)
    ]


def share(block, axis, groups):
    pieces = [block]
    for step in range(1, len(groups[0])):
        route = [(g[i], g[i ^ step]) for g in groups for i in range(len(g))]
        pieces.append(lax.ppermute(block, axis, route))
    return pieces


def dot(a, b):
    return jnp.dot(a, b, preferred_element_type=jnp.float32)


def dot_t(a, b):
    return lax.dot_general(a, b, (((1,), (1,)), ((), ())), preferred_element_type=jnp.float32)


def picked_rows(c, mid, far, mid_rows, seq_count):
    last = (c >= mid_rows) & (c < mid_rows + 4)
    other = jnp.where(last, (c - mid_rows) * seq_count + far, -1)
    return jnp.where(c < mid_rows, c * SPAN + mid, other)


def load_and_project(index, tok_hbm, w_hbm, tok_ref, w_ref, sems):
    deep = w_ref.shape[2]
    copies = {}
    count = 0
    for i, c in enumerate(index):
        for k in range(w_ref.shape[1]):
            rows = pl.ds(k * deep, deep)
            if i == 0:
                copies["t", k] = pltpu.make_async_copy(
                    tok_hbm.at[:, rows], tok_ref.at[k], sems.at[count]
                )
                count += 1
            copies[i, k] = pltpu.make_async_copy(
                w_hbm.at[c, rows], w_ref.at[i, k], sems.at[count]
            )
            count += 1
    for copy in copies.values():
        copy.start()

    def product(i):
        total = None
        for k in range(w_ref.shape[1]):
            if i == 0:
                copies["t", k].wait()
            copies[i, k].wait()
            part = dot(tok_ref[k], w_ref[i, k])
            total = part if total is None else total + part
        return total.astype(jnp.bfloat16)

    return product


def row_marks(mid, far, rows, seq_count):
    c = lax.broadcasted_iota(jnp.int32, (PICKS, rows), 0)
    r = lax.broadcasted_iota(jnp.int32, (PICKS, rows), 1)
    target = picked_rows(c, mid, far, rows // SPAN, seq_count)
    return jnp.where(r == target, 1.0, 0.0).astype(jnp.bfloat16)


def offset_copies(mid_hbm, far_hbm, mid_ref, far_ref, off_sems):
    offsets = [
        pltpu.make_async_copy(mid_hbm, mid_ref, off_sems.at[0]),
        pltpu.make_async_copy(far_hbm, far_ref, off_sems.at[1]),
    ]
    for copy in offsets:
        copy.start()
    return offsets


def kv_kernel(rows, heads, size, seq_count, mid_hbm, far_hbm, tok_hbm, w_hbm,
              kv_ref, mid_out, far_out, tok_ref, w_ref, few_ref, mid_ref, far_ref, off_sems, sems):
    offsets = offset_copies(mid_hbm, far_hbm, mid_ref, far_ref, off_sems)
    product = load_and_project((1, 2), tok_hbm, w_hbm, tok_ref, w_ref, sems)
    for copy in offsets:
        copy.wait()
    mid_rows = rows // SPAN
    marks = [row_marks(mid_ref[h], far_ref[h], rows, seq_count) for h in range(heads)]
    for c in range(2):
        whole = product(c)
        kv_ref[c] = whole
        for h in range(heads):
            got = dot(marks[h], whole[:, h * size : (h + 1) * size])
            for j in range(mid_out.shape[0]):
                mid_out[j, c, h] = got[:mid_rows].astype(jnp.bfloat16)
            few_ref[pl.ds(4 * h, 4)] = got[mid_rows : mid_rows + 4]
        few = few_ref[...].astype(jnp.bfloat16)
        for j in range(far_out.shape[0]):
            far_out[j, c] = few


def near_kernel(rows, heads, size, seq_count, mid_hbm, far_hbm, tok_hbm, w_hbm, kv_ref,
                near_ref, sel_ref, tok_ref, w_ref, mid_ref, far_ref, off_sems, sems):
    offsets = offset_copies(mid_hbm, far_hbm, mid_ref, far_ref, off_sems)
    product = load_and_project((0,), tok_hbm, w_hbm, tok_ref, w_ref, sems)
    whole = product(0)
    for copy in offsets:
        copy.wait()
    for h in range(heads):
        cols = slice(h * size, (h + 1) * size)
        queries = whole[:, cols]
        marks = row_marks(mid_ref[h], far_ref[h], rows, seq_count)
        sel_ref[h] = dot(marks, queries).astype(jnp.bfloat16)
        scores = dot_t(queries, kv_ref[0, :, cols]) * size**-0.5
        top = jnp.max(scores, axis=1, keepdims=True)
        weights = jnp.exp(scores - top)
        total = jnp.sum(weights, axis=1, keepdims=True)
        summed = dot(weights.astype(jnp.bfloat16), kv_ref[1, :, cols])
        near_ref[:, cols] = (summed / total).astype(jnp.bfloat16)


def softmax_parts(scores, values):
    top = jnp.max(scores, axis=1, keepdims=True)
    weights = jnp.exp(scores - top)
    total = jnp.sum(weights, axis=1, keepdims=True)
    return top, total, dot(weights.astype(jnp.bfloat16), values)


def wide_kernel(rows, heads, size, seq_count, quarters,
                mid_hbm, far_hbm, place_ref, sel_ref, kv_ref, near_ref, *refs):
    mid_lines, far_lines, w_hbm = refs[0:2], refs[2:4], refs[4]
    outs, attn_ref = refs[5 : 5 + quarters], refs[5 + quarters]
    mid_ref, far_ref, off_sems, w_ref, w_sem = refs[6 + quarters :]
    offsets = offset_copies(mid_hbm, far_hbm, mid_ref, far_ref, off_sems)
    w_copy = pltpu.make_async_copy(w_hbm, w_ref, w_sem)
    w_copy.start()
    mid_rows = rows // SPAN
    scale = size**-0.5
    far_rows = lambda i: jnp.concatenate([ref[:, i].reshape(-1, size) for ref in far_lines])
    far_q = jnp.concatenate([sel_ref[h].astype(jnp.float32)[mid_rows:] for h in range(heads)])
    far_scores = dot_t(far_q.astype(jnp.bfloat16), far_rows(0)) * scale
    q_head = lax.broadcasted_iota(jnp.int32, far_scores.shape, 0) // 8
    k_head = (lax.broadcasted_iota(jnp.int32, far_scores.shape, 1) % 16) // 4
    far_top, far_total, far_sum = softmax_parts(
        jnp.where(q_head == k_head, far_scores, LOW), far_rows(1)
    )
    for copy in offsets:
        copy.wait()
    for h in range(heads):
        cols = slice(h * size, (h + 1) * size)
        mid_off, far_off = mid_ref[h], far_ref[h]
        stack = lambda i: jnp.concatenate(
            [kv_ref[i, :, cols]] + [ref[:, i, h].reshape(-1, size) for ref in mid_lines]
        )
        scores = dot_t(sel_ref[h], stack(0)) * scale
        row = lax.broadcasted_iota(jnp.int32, scores.shape, 0)
        col = lax.broadcasted_iota(jnp.int32, scores.shape, 1)
        both = ((far_off + SPAN - mid_off) & (SPAN - 1)) == 0
        keep = (row < mid_rows) | (col < rows) | both
        top, total, summed = softmax_parts(jnp.where(keep, scores, LOW), stack(1))
        attn = summed / total
        far = slice(8 * h, 8 * h + 8)
        peak = jnp.maximum(top[mid_rows:], far_top[far])
        mine = jnp.exp(top[mid_rows:] - peak)
        other = jnp.exp(far_top[far] - peak)
        attn_far = (mine * summed[mid_rows:] + other * far_sum[far]) / (
            mine * total[mid_rows:] + other * far_total[far]
        )
        attn = jnp.concatenate([attn[:mid_rows], attn_far]).astype(jnp.bfloat16)
        r = lax.broadcasted_iota(jnp.int32, (rows, PICKS), 0)
        c = lax.broadcasted_iota(jnp.int32, (rows, PICKS), 1)
        target = picked_rows(c, mid_off, far_off, mid_rows, seq_count)
        twice = (c < mid_rows) & (
            ((target + seq_count - far_off) & (seq_count - 1)) == 0
        )
        marks = jnp.where((r == target) & jnp.logical_not(twice), 1.0, 0.0)
        hit = jnp.sum(marks, axis=1, keepdims=True) > 0.5
        put = dot(marks.astype(jnp.bfloat16), attn)
        attn_ref[:, cols] = jnp.where(hit, put, near_ref[:, cols].astype(jnp.float32))
    own = rows // quarters
    place = place_ref[0]
    order = jnp.concatenate(
        [
            attn_ref[pl.ds(pl.multiple_of((place ^ s) * own, own), own), :]
            for s in range(quarters)
        ]
    ).astype(jnp.bfloat16)
    w_copy.wait()
    chunk = 512
    for start in range(0, w_ref.shape[1], chunk):
        part = dot(order, w_ref[:, start : start + chunk]).astype(jnp.bfloat16)
        for s in range(quarters):
            outs[s][:, start : start + chunk] = part[s * own : (s + 1) * own]


def logits_kernel(place_ref, tok_ref, gain_ref, label_ref, *refs):
    out_ref = refs[-1]
    mixed = tok_ref[...].astype(jnp.float32)
    for ref in refs[:-1]:
        mixed = mixed + ref[...].astype(jnp.float32)
    mean_sq = jnp.mean(mixed * mixed, axis=1, keepdims=True)
    scaled = (mixed * gain_ref[...]).astype(jnp.bfloat16)
    out_ref[...] = dot(scaled, label_ref[...]) / jnp.sqrt(mean_sq + 1e-05)


def body(tokens, w_qkv, w_out, norm_gain, w_label, offset_mid, offset_far):
    rows, width = tokens.shape
    heads = offset_mid.shape[0]
    cols = w_qkv.shape[2]
    size = cols // heads
    seq_count = lax.axis_size("seq")
    head_count = lax.axis_size("head")
    place = lax.axis_index("head")
    mid_rows = rows // SPAN
    sizes = (rows, heads, size, seq_count)
    bf16 = lambda *shape: jax.ShapeDtypeStruct(shape, jnp.bfloat16)
    stay = lambda a: pltpu.with_memory_space_constraint(a, pltpu.HBM)
    tokens, weights = stay(tokens), stay(w_qkv.transpose(1, 0, 2))
    offset_mid, offset_far, w_out = stay(offset_mid), stay(offset_far), stay(w_out)
    deep = 512

    groups = segments(seq_count)
    across = [[g[2 * i + c] for i in range(SPAN // 2)] for g in groups for c in range(2)]
    chips = [list(range(c, seq_count, 2)) for c in range(2)]
    cores = [(i, i ^ 1) for i in range(seq_count)]
    near_count, far_count = len(across[0]), len(chips[0])
    steps = width // deep
    tok_scratch = pltpu.VMEM((steps, rows, deep), jnp.bfloat16)

    off_scratch = [
        pltpu.SMEM((heads,), jnp.int32),
        pltpu.SMEM((heads,), jnp.int32),
        pltpu.SemaphoreType.DMA((2,)),
    ]

    kv, mid_kv, far_kv = pl.pallas_call(
        functools.partial(kv_kernel, *sizes),
        in_specs=[HBM] * 4,
        out_specs=[VMEM] * 3,
        out_shape=[
            bf16(2, rows, cols),
            bf16(1, 2, heads, mid_rows, size),
            bf16(far_count, 2, 4 * heads, size),
        ],
        scratch_shapes=[
            tok_scratch,
            pltpu.VMEM((2, steps, deep, cols), jnp.bfloat16),
            pltpu.VMEM((4 * heads, size), jnp.float32),
            *off_scratch,
            pltpu.SemaphoreType.DMA((3 * steps,)),
        ],
        compiler_params=params(20),
        name="keys_values",
    )(offset_mid, offset_far, tokens, weights)

    far_line = lax.all_to_all(far_kv, "seq", 0, 0, axis_index_groups=chips)
    mid_pieces = share(mid_kv[0], "seq", across)
    near, sel = pl.pallas_call(
        functools.partial(near_kernel, *sizes),
        in_specs=[HBM] * 4 + [VMEM],
        out_specs=[VMEM] * 2,
        out_shape=[bf16(rows, cols), bf16(heads, PICKS, size)],
        scratch_shapes=[
            tok_scratch,
            pltpu.VMEM((1, steps, deep, cols), jnp.bfloat16),
            *off_scratch,
            pltpu.SemaphoreType.DMA((2 * steps,)),
        ],
        compiler_params=params(14),
        name="near",
    )(offset_mid, offset_far, tokens, weights, kv)

    *mid_pieces, near = lax.optimization_barrier((*mid_pieces, near))
    mid_line = jnp.stack(mid_pieces)
    mid_other = lax.ppermute(mid_line, "seq", cores)
    far_other = lax.ppermute(far_line, "seq", cores)

    own = rows // head_count
    place_arr = place.astype(jnp.int32).reshape(1)
    parts = pl.pallas_call(
        functools.partial(wide_kernel, *sizes, head_count),
        in_specs=[HBM, HBM, SMEM] + [VMEM] * 7 + [HBM],
        out_specs=[VMEM] * head_count,
        out_shape=[bf16(own, width)] * head_count,
        scratch_shapes=[
            pltpu.VMEM((rows, cols), jnp.float32),
            *off_scratch,
            pltpu.VMEM(w_out.shape, jnp.bfloat16),
            pltpu.SemaphoreType.DMA,
        ],
        compiler_params=params(14),
        name="wide",
    )(
        offset_mid, offset_far, place_arr, sel, kv, near,
        mid_line, mid_other, far_line, far_other, w_out,
    )

    got = [parts[0]]
    for step in range(1, head_count):
        route = [(i, i ^ step) for i in range(head_count)]
        got.append(lax.ppermute(parts[step], "head", route))

    whole = lambda *shape: pl.BlockSpec(shape, lambda i, p: (0,) * len(shape))
    logit = pl.pallas_call(
        logits_kernel,
        grid_spec=pltpu.PrefetchScalarGridSpec(
            num_scalar_prefetch=1,
            grid=(1,),
            in_specs=[
                pl.BlockSpec((own, width), lambda i, p: (p[0], 0)),
                whole(1, width),
                whole(*w_label.shape),
            ]
            + [whole(own, width)] * head_count,
            out_specs=whole(own, w_label.shape[1]),
        ),
        out_shape=jax.ShapeDtypeStruct((own, w_label.shape[1]), jnp.float32),
        compiler_params=params(10),
        name="logits",
    )(place_arr, tokens, norm_gain.reshape(1, width), w_label, *got)

    every = share(logit, "head", [list(range(head_count))])
    logits = jnp.zeros((head_count,) + logit.shape, jnp.float32)
    for step in range(head_count):
        logits = lax.dynamic_update_index_in_dim(logits, every[step], place ^ step, 0)
    return logits.reshape(rows, -1)


def solution(mesh):
    return jax.shard_map(
        body,
        mesh=mesh,
        in_specs=(
            P("seq", None),
            P(None, None, "head"),
            P("head", None),
            P(),
            P(),
            P("head"),
            P("head"),
        ),
        out_specs=P("seq", None),
        check_vma=False,
    )
```

```python
import functools

import jax
import jax.numpy as jnp
from jax import lax
from jax.experimental import pallas as pl
from jax.experimental.pallas import tpu as pltpu
from jax.sharding import PartitionSpec as P

SPAN = 8
PICKS = 40
LOW = -1e30
HALVING = (((0, 3), (1, 2)), ((0, 1), (3, 2)))
VMEM = pl.BlockSpec(memory_space=pltpu.VMEM)
HBM = pl.BlockSpec(memory_space=pltpu.HBM)
SMEM = pl.BlockSpec(memory_space=pltpu.SMEM)


def params(mib):
    return pltpu.CompilerParams(vmem_limit_bytes=mib << 20)


def segments(seq_count):
    return [
        [(SPAN * k - SPAN // 2 + i) % seq_count for i in range(SPAN)]
        for k in range(seq_count // SPAN)
    ]


def share(block, axis, groups):
    pieces = [block]
    for step in range(1, len(groups[0])):
        route = [(g[i], g[i ^ step]) for g in groups for i in range(len(g))]
        pieces.append(lax.ppermute(block, axis, route))
    return pieces


def dot(a, b):
    return jnp.dot(a, b, preferred_element_type=jnp.float32)


def dot_t(a, b):
    return lax.dot_general(a, b, (((1,), (1,)), ((), ())), preferred_element_type=jnp.float32)


def picked_rows(c, mid, far, mid_rows, seq_count):
    last = (c >= mid_rows) & (c < mid_rows + 4)
    other = jnp.where(last, (c - mid_rows) * seq_count + far, -1)
    return jnp.where(c < mid_rows, c * SPAN + mid, other)


def load_and_project(index, tok_hbm, w_hbm, tok_ref, w_ref, sems):
    deep = w_ref.shape[2]
    copies = {}
    count = 0
    for i, c in enumerate(index):
        for k in range(w_ref.shape[1]):
            rows = pl.ds(k * deep, deep)
            if i == 0:
                copies["t", k] = pltpu.make_async_copy(
                    tok_hbm.at[:, rows], tok_ref.at[k], sems.at[count]
                )
                count += 1
            copies[i, k] = pltpu.make_async_copy(
                w_hbm.at[c, rows], w_ref.at[i, k], sems.at[count]
            )
            count += 1
    for copy in copies.values():
        copy.start()

    def product(i):
        total = None
        for k in range(w_ref.shape[1]):
            if i == 0:
                copies["t", k].wait()
            copies[i, k].wait()
            part = dot(tok_ref[k], w_ref[i, k])
            total = part if total is None else total + part
        return total.astype(jnp.bfloat16)

    return product


def row_marks(mid, far, rows, seq_count):
    c = lax.broadcasted_iota(jnp.int32, (PICKS, rows), 0)
    r = lax.broadcasted_iota(jnp.int32, (PICKS, rows), 1)
    target = picked_rows(c, mid, far, rows // SPAN, seq_count)
    return jnp.where(r == target, 1.0, 0.0).astype(jnp.bfloat16)


def offset_copies(mid_hbm, far_hbm, mid_ref, far_ref, off_sems):
    offsets = [
        pltpu.make_async_copy(mid_hbm, mid_ref, off_sems.at[0]),
        pltpu.make_async_copy(far_hbm, far_ref, off_sems.at[1]),
    ]
    for copy in offsets:
        copy.start()
    return offsets


def kv_kernel(rows, heads, size, seq_count, mid_hbm, far_hbm, tok_hbm, w_hbm,
              kv_ref, mid_out, far_out, tok_ref, w_ref, few_ref, mid_ref, far_ref, off_sems, sems):
    offsets = offset_copies(mid_hbm, far_hbm, mid_ref, far_ref, off_sems)
    product = load_and_project((1, 2), tok_hbm, w_hbm, tok_ref, w_ref, sems)
    for copy in offsets:
        copy.wait()
    mid_rows = rows // SPAN
    marks = [row_marks(mid_ref[h], far_ref[h], rows, seq_count) for h in range(heads)]
    for c in range(2):
        whole = product(c)
        kv_ref[c] = whole
        for h in range(heads):
            got = dot(marks[h], whole[:, h * size : (h + 1) * size])
            for j in range(mid_out.shape[0]):
                mid_out[j, c, h] = got[:mid_rows].astype(jnp.bfloat16)
            few_ref[pl.ds(4 * h, 4)] = got[mid_rows : mid_rows + 4]
        few = few_ref[...].astype(jnp.bfloat16)
        for j in range(far_out.shape[0]):
            far_out[j, c] = few


def near_kernel(rows, heads, size, seq_count, mid_hbm, far_hbm, tok_hbm, w_hbm, kv_ref,
                near_ref, sel_ref, tok_ref, w_ref, mid_ref, far_ref, off_sems, sems):
    offsets = offset_copies(mid_hbm, far_hbm, mid_ref, far_ref, off_sems)
    product = load_and_project((0,), tok_hbm, w_hbm, tok_ref, w_ref, sems)
    whole = product(0)
    for copy in offsets:
        copy.wait()
    for h in range(heads):
        cols = slice(h * size, (h + 1) * size)
        queries = whole[:, cols]
        marks = row_marks(mid_ref[h], far_ref[h], rows, seq_count)
        sel_ref[h] = dot(marks, queries).astype(jnp.bfloat16)
        scores = dot_t(queries, kv_ref[0, :, cols]) * size**-0.5
        top = jnp.max(scores, axis=1, keepdims=True)
        weights = jnp.exp(scores - top)
        total = jnp.sum(weights, axis=1, keepdims=True)
        summed = dot(weights.astype(jnp.bfloat16), kv_ref[1, :, cols])
        near_ref[:, cols] = (summed / total).astype(jnp.bfloat16)


def softmax_parts(scores, values):
    top = jnp.max(scores, axis=1, keepdims=True)
    weights = jnp.exp(scores - top)
    total = jnp.sum(weights, axis=1, keepdims=True)
    return top, total, dot(weights.astype(jnp.bfloat16), values)


def wide_kernel(rows, heads, size, seq_count, quarters,
                mid_hbm, far_hbm, place_ref, sel_ref, kv_ref, near_ref, *refs):
    mid_lines, far_lines, w_hbm = refs[0:2], refs[2:4], refs[4]
    outs, refs = refs[5:9], refs[9:]
    attn_ref, mid_ref, far_ref, off_sems, w_ref, w_sem = refs
    offsets = offset_copies(mid_hbm, far_hbm, mid_ref, far_ref, off_sems)
    w_copy = pltpu.make_async_copy(w_hbm, w_ref, w_sem)
    w_copy.start()
    mid_rows = rows // SPAN
    scale = size**-0.5
    far_rows = lambda i: jnp.concatenate([ref[:, i].reshape(-1, size) for ref in far_lines])
    far_q = jnp.concatenate([sel_ref[h].astype(jnp.float32)[mid_rows:] for h in range(heads)])
    far_scores = dot_t(far_q.astype(jnp.bfloat16), far_rows(0)) * scale
    q_head = lax.broadcasted_iota(jnp.int32, far_scores.shape, 0) // 8
    k_head = (lax.broadcasted_iota(jnp.int32, far_scores.shape, 1) % 16) // 4
    far_top, far_total, far_sum = softmax_parts(
        jnp.where(q_head == k_head, far_scores, LOW), far_rows(1)
    )
    for copy in offsets:
        copy.wait()
    for h in range(heads):
        cols = slice(h * size, (h + 1) * size)
        mid_off, far_off = mid_ref[h], far_ref[h]
        stack = lambda i: jnp.concatenate(
            [kv_ref[i, :, cols]] + [ref[:, i, h].reshape(-1, size) for ref in mid_lines]
        )
        scores = dot_t(sel_ref[h], stack(0)) * scale
        row = lax.broadcasted_iota(jnp.int32, scores.shape, 0)
        col = lax.broadcasted_iota(jnp.int32, scores.shape, 1)
        both = ((far_off + SPAN - mid_off) & (SPAN - 1)) == 0
        keep = (row < mid_rows) | (col < rows) | both
        top, total, summed = softmax_parts(jnp.where(keep, scores, LOW), stack(1))
        attn = summed / total
        far = slice(8 * h, 8 * h + 8)
        peak = jnp.maximum(top[mid_rows:], far_top[far])
        mine = jnp.exp(top[mid_rows:] - peak)
        other = jnp.exp(far_top[far] - peak)
        attn_far = (mine * summed[mid_rows:] + other * far_sum[far]) / (
            mine * total[mid_rows:] + other * far_total[far]
        )
        attn = jnp.concatenate([attn[:mid_rows], attn_far]).astype(jnp.bfloat16)
        r = lax.broadcasted_iota(jnp.int32, (rows, PICKS), 0)
        c = lax.broadcasted_iota(jnp.int32, (rows, PICKS), 1)
        target = picked_rows(c, mid_off, far_off, mid_rows, seq_count)
        twice = (c < mid_rows) & (
            ((target + seq_count - far_off) & (seq_count - 1)) == 0
        )
        marks = jnp.where((r == target) & jnp.logical_not(twice), 1.0, 0.0)
        hit = jnp.sum(marks, axis=1, keepdims=True) > 0.5
        put = dot(marks.astype(jnp.bfloat16), attn)
        attn_ref[:, cols] = jnp.where(hit, put, near_ref[:, cols].astype(jnp.float32))
    own = rows // quarters
    place = place_ref[0]
    order = jnp.concatenate(
        [
            attn_ref[pl.ds(pl.multiple_of((place ^ s) * own, own), own), :]
            for s in range(quarters)
        ]
    ).astype(jnp.bfloat16)
    w_copy.wait()
    half = w_ref.shape[1] // 2
    chunk = 512
    for start in range(0, 2 * half, chunk):
        part = dot(order, w_ref[:, start : start + chunk]).astype(jnp.bfloat16)
        side = start // half
        to = slice(start % half, start % half + chunk)
        for name, taken in enumerate(HALVING[side]):
            for i, s in enumerate(taken):
                outs[2 * side + name][i * own : (i + 1) * own, to] = part[s * own : (s + 1) * own]


def logits_kernel(place_ref, tok_ref, gain_ref, label_ref, *refs):
    out_ref = refs[-1]
    own, width = tok_ref.shape
    half = width // 2
    square = jnp.zeros((own, 1), jnp.float32)
    product = jnp.zeros(out_ref.shape, jnp.float32)
    for side in range(2):
        cols = slice(side * half, (side + 1) * half)
        mixed = tok_ref[:, cols].astype(jnp.float32)
        for ref in refs[3 * side : 3 * side + 3]:
            mixed = mixed + ref[:own].astype(jnp.float32)
        square = square + jnp.sum(mixed * mixed, axis=1, keepdims=True)
        scaled = (mixed * gain_ref[:, cols]).astype(jnp.bfloat16)
        product = product + dot(scaled, label_ref[cols])
    out_ref[...] = product / jnp.sqrt(square / width + 1e-05)


def body(tokens, w_qkv, w_out, norm_gain, w_label, offset_mid, offset_far):
    rows, width = tokens.shape
    heads = offset_mid.shape[0]
    cols = w_qkv.shape[2]
    size = cols // heads
    seq_count = lax.axis_size("seq")
    head_count = lax.axis_size("head")
    place = lax.axis_index("head")
    mid_rows = rows // SPAN
    sizes = (rows, heads, size, seq_count)
    bf16 = lambda *shape: jax.ShapeDtypeStruct(shape, jnp.bfloat16)
    stay = lambda a: pltpu.with_memory_space_constraint(a, pltpu.HBM)
    tokens, weights = stay(tokens), stay(w_qkv.transpose(1, 0, 2))
    offset_mid, offset_far, w_out = stay(offset_mid), stay(offset_far), stay(w_out)
    deep = 512

    groups = segments(seq_count)
    across = [[g[2 * i + c] for i in range(SPAN // 2)] for g in groups for c in range(2)]
    chips = [list(range(c, seq_count, 2)) for c in range(2)]
    cores = [(i, i ^ 1) for i in range(seq_count)]
    near_count, far_count = len(across[0]), len(chips[0])
    steps = width // deep
    tok_scratch = pltpu.VMEM((steps, rows, deep), jnp.bfloat16)

    off_scratch = [
        pltpu.SMEM((heads,), jnp.int32),
        pltpu.SMEM((heads,), jnp.int32),
        pltpu.SemaphoreType.DMA((2,)),
    ]

    kv, mid_kv, far_kv = pl.pallas_call(
        functools.partial(kv_kernel, *sizes),
        in_specs=[HBM] * 4,
        out_specs=[VMEM] * 3,
        out_shape=[
            bf16(2, rows, cols),
            bf16(1, 2, heads, mid_rows, size),
            bf16(far_count, 2, 4 * heads, size),
        ],
        scratch_shapes=[
            tok_scratch,
            pltpu.VMEM((2, steps, deep, cols), jnp.bfloat16),
            pltpu.VMEM((4 * heads, size), jnp.float32),
            *off_scratch,
            pltpu.SemaphoreType.DMA((3 * steps,)),
        ],
        compiler_params=params(20),
        name="keys_values",
    )(offset_mid, offset_far, tokens, weights)

    far_line = lax.all_to_all(far_kv, "seq", 0, 0, axis_index_groups=chips)
    mid_pieces = share(mid_kv[0], "seq", across)
    near, sel = pl.pallas_call(
        functools.partial(near_kernel, *sizes),
        in_specs=[HBM] * 4 + [VMEM],
        out_specs=[VMEM] * 2,
        out_shape=[bf16(rows, cols), bf16(heads, PICKS, size)],
        scratch_shapes=[
            tok_scratch,
            pltpu.VMEM((1, steps, deep, cols), jnp.bfloat16),
            *off_scratch,
            pltpu.SemaphoreType.DMA((2 * steps,)),
        ],
        compiler_params=params(14),
        name="near",
    )(offset_mid, offset_far, tokens, weights, kv)

    *mid_pieces, near = lax.optimization_barrier((*mid_pieces, near))
    mid_line = jnp.stack(mid_pieces)
    mid_other = lax.ppermute(mid_line, "seq", cores)
    far_other = lax.ppermute(far_line, "seq", cores)

    own = rows // head_count
    place_arr = place.astype(jnp.int32).reshape(1)
    half = width // 2
    kept_a, sent_a, kept_b, sent_b = pl.pallas_call(
        functools.partial(wide_kernel, *sizes, head_count),
        in_specs=[HBM, HBM, SMEM] + [VMEM] * 7 + [HBM],
        out_specs=[VMEM] * 4,
        out_shape=[bf16(2 * own, half)] * 4,
        scratch_shapes=[
            pltpu.VMEM((rows, cols), jnp.float32),
            *off_scratch,
            pltpu.VMEM(w_out.shape, jnp.bfloat16),
            pltpu.SemaphoreType.DMA,
        ],
        compiler_params=params(14),
        name="wide",
    )(
        offset_mid, offset_far, place_arr, sel, kv, near,
        mid_line, mid_other, far_line, far_other, w_out,
    )

    swap = lambda a, step: lax.ppermute(a, "head", [(i, i ^ step) for i in range(head_count)])
    got_a, got_b = swap(sent_a, 1), swap(sent_b, 3)
    tail = lambda a: a[own:].astype(jnp.float32)
    last_a = swap((tail(kept_a) + tail(got_a)).astype(jnp.bfloat16), 3)
    last_b = swap((tail(kept_b) + tail(got_b)).astype(jnp.bfloat16), 1)
    got = [kept_a, got_a, last_a, kept_b, got_b, last_b]

    whole = lambda *shape: pl.BlockSpec(shape, lambda i, p: (0,) * len(shape))
    logit = pl.pallas_call(
        logits_kernel,
        grid_spec=pltpu.PrefetchScalarGridSpec(
            num_scalar_prefetch=1,
            grid=(1,),
            in_specs=[
                pl.BlockSpec((own, width), lambda i, p: (p[0], 0)),
                whole(1, width),
                whole(*w_label.shape),
            ]
            + [whole(own, half)] * len(got),
            out_specs=whole(own, w_label.shape[1]),
        ),
        out_shape=jax.ShapeDtypeStruct((own, w_label.shape[1]), jnp.float32),
        compiler_params=params(10),
        name="logits",
    )(place_arr, tokens, norm_gain.reshape(1, width), w_label, *got)

    every = share(logit, "head", [list(range(head_count))])
    logits = jnp.zeros((head_count,) + logit.shape, jnp.float32)
    for step in range(head_count):
        logits = lax.dynamic_update_index_in_dim(logits, every[step], place ^ step, 0)
    return logits.reshape(rows, -1)


def solution(mesh):
    return jax.shard_map(
        body,
        mesh=mesh,
        in_specs=(
            P("seq", None),
            P(None, None, "head"),
            P("head", None),
            P(),
            P(),
            P("head"),
            P("head"),
        ),
        out_specs=P("seq", None),
        check_vma=False,
    )
```

```python
import functools

import jax
import jax.numpy as jnp
from jax import lax
from jax.experimental import pallas as pl
from jax.experimental.pallas import tpu as pltpu
from jax.sharding import PartitionSpec as P

SPAN = 8
PICKS = 40
LOW = -1e30
HALVING = (((0, 3), (1, 2)), ((0, 1), (3, 2)))
VMEM = pl.BlockSpec(memory_space=pltpu.VMEM)
HBM = pl.BlockSpec(memory_space=pltpu.HBM)
SMEM = pl.BlockSpec(memory_space=pltpu.SMEM)


def params(mib):
    return pltpu.CompilerParams(vmem_limit_bytes=mib << 20)


def segments(seq_count):
    return [
        [(SPAN * k - SPAN // 2 + i) % seq_count for i in range(SPAN)]
        for k in range(seq_count // SPAN)
    ]


def share(block, axis, groups):
    pieces = [block]
    for step in range(1, len(groups[0])):
        route = [(g[i], g[i ^ step]) for g in groups for i in range(len(g))]
        pieces.append(lax.ppermute(block, axis, route))
    return pieces


def dot(a, b):
    return jnp.dot(a, b, preferred_element_type=jnp.float32)


def dot_t(a, b):
    return lax.dot_general(a, b, (((1,), (1,)), ((), ())), preferred_element_type=jnp.float32)


def picked_rows(c, mid, far, mid_rows, seq_count):
    last = (c >= mid_rows) & (c < mid_rows + 4)
    other = jnp.where(last, (c - mid_rows) * seq_count + far, -1)
    return jnp.where(c < mid_rows, c * SPAN + mid, other)


def load_and_project(index, tok_hbm, w_hbm, tok_ref, w_ref, sems):
    deep = w_ref.shape[2]
    copies = {}
    count = 0
    for i, c in enumerate(index):
        for k in range(w_ref.shape[1]):
            rows = pl.ds(k * deep, deep)
            if i == 0:
                copies["t", k] = pltpu.make_async_copy(
                    tok_hbm.at[:, rows], tok_ref.at[k], sems.at[count]
                )
                count += 1
            copies[i, k] = pltpu.make_async_copy(
                w_hbm.at[c, rows], w_ref.at[i, k], sems.at[count]
            )
            count += 1
    for copy in copies.values():
        copy.start()

    def product(i):
        total = None
        for k in range(w_ref.shape[1]):
            if i == 0:
                copies["t", k].wait()
            copies[i, k].wait()
            part = dot(tok_ref[k], w_ref[i, k])
            total = part if total is None else total + part
        return total.astype(jnp.bfloat16)

    return product


def row_marks(mid, far, rows, seq_count):
    c = lax.broadcasted_iota(jnp.int32, (PICKS, rows), 0)
    r = lax.broadcasted_iota(jnp.int32, (PICKS, rows), 1)
    target = picked_rows(c, mid, far, rows // SPAN, seq_count)
    return jnp.where(r == target, 1.0, 0.0).astype(jnp.bfloat16)


def offset_copies(mid_hbm, far_hbm, mid_ref, far_ref, off_sems):
    offsets = [
        pltpu.make_async_copy(mid_hbm, mid_ref, off_sems.at[0]),
        pltpu.make_async_copy(far_hbm, far_ref, off_sems.at[1]),
    ]
    for copy in offsets:
        copy.start()
    return offsets


def kv_kernel(rows, heads, size, seq_count, mid_hbm, far_hbm, tok_hbm, w_hbm,
              kv_ref, mid_out, far_out, tok_ref, w_ref, few_ref, mid_ref, far_ref, off_sems, sems):
    offsets = offset_copies(mid_hbm, far_hbm, mid_ref, far_ref, off_sems)
    product = load_and_project((1, 2), tok_hbm, w_hbm, tok_ref, w_ref, sems)
    for copy in offsets:
        copy.wait()
    mid_rows = rows // SPAN
    marks = [row_marks(mid_ref[h], far_ref[h], rows, seq_count) for h in range(heads)]
    for c in range(2):
        whole = product(c)
        kv_ref[c] = whole
        for h in range(heads):
            got = dot(marks[h], whole[:, h * size : (h + 1) * size])
            for j in range(mid_out.shape[0]):
                mid_out[j, c, h] = got[:mid_rows].astype(jnp.bfloat16)
            few_ref[pl.ds(4 * h, 4)] = got[mid_rows : mid_rows + 4]
        few = few_ref[...].astype(jnp.bfloat16)
        for j in range(far_out.shape[0]):
            far_out[j, c] = few


def near_kernel(rows, heads, size, seq_count, mid_hbm, far_hbm, place_ref, tok_hbm, w_hbm, kv_ref,
                near_ref, sel_ref, own_ref, tok_ref, w_ref, mid_ref, far_ref, off_sems, sems):
    offsets = offset_copies(mid_hbm, far_hbm, mid_ref, far_ref, off_sems)
    product = load_and_project((0,), tok_hbm, w_hbm, tok_ref, w_ref, sems)
    whole = product(0)
    own, deep = own_ref.shape[0], tok_ref.shape[2]
    mine = pl.ds(pl.multiple_of(place_ref[0] * own, own), own)
    for k in range(tok_ref.shape[0]):
        own_ref[:, k * deep : (k + 1) * deep] = tok_ref[k, mine, :]
    for copy in offsets:
        copy.wait()
    for h in range(heads):
        cols = slice(h * size, (h + 1) * size)
        queries = whole[:, cols]
        marks = row_marks(mid_ref[h], far_ref[h], rows, seq_count)
        sel_ref[h] = dot(marks, queries).astype(jnp.bfloat16)
        scores = dot_t(queries, kv_ref[0, :, cols]) * size**-0.5
        top = jnp.max(scores, axis=1, keepdims=True)
        weights = jnp.exp(scores - top)
        total = jnp.sum(weights, axis=1, keepdims=True)
        summed = dot(weights.astype(jnp.bfloat16), kv_ref[1, :, cols])
        near_ref[:, cols] = (summed / total).astype(jnp.bfloat16)


def softmax_parts(scores, values):
    top = jnp.max(scores, axis=1, keepdims=True)
    weights = jnp.exp(scores - top)
    total = jnp.sum(weights, axis=1, keepdims=True)
    return top, total, dot(weights.astype(jnp.bfloat16), values)


def wide_kernel(rows, heads, size, seq_count, quarters,
                mid_hbm, far_hbm, place_ref, sel_ref, kv_ref, near_ref, *refs):
    mid_lines, far_lines, w_hbm = refs[0:2], refs[2:4], refs[4]
    outs, refs = refs[5:9], refs[9:]
    attn_ref, mid_ref, far_ref, off_sems, w_ref, w_sem = refs
    offsets = offset_copies(mid_hbm, far_hbm, mid_ref, far_ref, off_sems)
    w_copy = pltpu.make_async_copy(w_hbm, w_ref, w_sem)
    w_copy.start()
    mid_rows = rows // SPAN
    scale = size**-0.5
    far_rows = lambda i: jnp.concatenate([ref[:, i].reshape(-1, size) for ref in far_lines])
    far_q = jnp.concatenate([sel_ref[h].astype(jnp.float32)[mid_rows:] for h in range(heads)])
    far_scores = dot_t(far_q.astype(jnp.bfloat16), far_rows(0)) * scale
    q_head = lax.broadcasted_iota(jnp.int32, far_scores.shape, 0) // 8
    k_head = (lax.broadcasted_iota(jnp.int32, far_scores.shape, 1) % 16) // 4
    far_top, far_total, far_sum = softmax_parts(
        jnp.where(q_head == k_head, far_scores, LOW), far_rows(1)
    )
    for copy in offsets:
        copy.wait()
    for h in range(heads):
        cols = slice(h * size, (h + 1) * size)
        mid_off, far_off = mid_ref[h], far_ref[h]
        stack = lambda i: jnp.concatenate(
            [kv_ref[i, :, cols]] + [ref[:, i, h].reshape(-1, size) for ref in mid_lines]
        )
        scores = dot_t(sel_ref[h], stack(0)) * scale
        row = lax.broadcasted_iota(jnp.int32, scores.shape, 0)
        col = lax.broadcasted_iota(jnp.int32, scores.shape, 1)
        both = ((far_off + SPAN - mid_off) & (SPAN - 1)) == 0
        keep = (row < mid_rows) | (col < rows) | both
        top, total, summed = softmax_parts(jnp.where(keep, scores, LOW), stack(1))
        attn = summed / total
        far = slice(8 * h, 8 * h + 8)
        peak = jnp.maximum(top[mid_rows:], far_top[far])
        mine = jnp.exp(top[mid_rows:] - peak)
        other = jnp.exp(far_top[far] - peak)
        attn_far = (mine * summed[mid_rows:] + other * far_sum[far]) / (
            mine * total[mid_rows:] + other * far_total[far]
        )
        attn = jnp.concatenate([attn[:mid_rows], attn_far]).astype(jnp.bfloat16)
        r = lax.broadcasted_iota(jnp.int32, (rows, PICKS), 0)
        c = lax.broadcasted_iota(jnp.int32, (rows, PICKS), 1)
        target = picked_rows(c, mid_off, far_off, mid_rows, seq_count)
        twice = (c < mid_rows) & (
            ((target + seq_count - far_off) & (seq_count - 1)) == 0
        )
        marks = jnp.where((r == target) & jnp.logical_not(twice), 1.0, 0.0)
        hit = jnp.sum(marks, axis=1, keepdims=True) > 0.5
        put = dot(marks.astype(jnp.bfloat16), attn)
        attn_ref[:, cols] = jnp.where(hit, put, near_ref[:, cols].astype(jnp.float32))
    own = rows // quarters
    place = place_ref[0]
    order = jnp.concatenate(
        [
            attn_ref[pl.ds(pl.multiple_of((place ^ s) * own, own), own), :]
            for s in range(quarters)
        ]
    ).astype(jnp.bfloat16)
    w_copy.wait()
    half = w_ref.shape[1] // 2
    chunk = 512
    for start in range(0, 2 * half, chunk):
        part = dot(order, w_ref[:, start : start + chunk]).astype(jnp.bfloat16)
        side = start // half
        to = slice(start % half, start % half + chunk)
        for name, taken in enumerate(HALVING[side]):
            for i, s in enumerate(taken):
                outs[2 * side + name][i * own : (i + 1) * own, to] = part[s * own : (s + 1) * own]


def logits_kernel(tok_ref, gain_ref, label_ref, *refs):
    out_ref = refs[-1]
    own, width = tok_ref.shape
    half = width // 2
    square = jnp.zeros((own, 1), jnp.float32)
    product = jnp.zeros(out_ref.shape, jnp.float32)
    for side in range(2):
        cols = slice(side * half, (side + 1) * half)
        mixed = tok_ref[:, cols].astype(jnp.float32)
        for ref in refs[3 * side : 3 * side + 3]:
            mixed = mixed + ref[:own].astype(jnp.float32)
        square = square + jnp.sum(mixed * mixed, axis=1, keepdims=True)
        scaled = (mixed * gain_ref[:, cols]).astype(jnp.bfloat16)
        product = product + dot(scaled, label_ref[cols])
    out_ref[...] = product / jnp.sqrt(square / width + 1e-05)


def body(tokens, w_qkv, w_out, norm_gain, w_label, offset_mid, offset_far):
    rows, width = tokens.shape
    heads = offset_mid.shape[0]
    cols = w_qkv.shape[2]
    size = cols // heads
    seq_count = lax.axis_size("seq")
    head_count = lax.axis_size("head")
    place = lax.axis_index("head")
    mid_rows = rows // SPAN
    sizes = (rows, heads, size, seq_count)
    bf16 = lambda *shape: jax.ShapeDtypeStruct(shape, jnp.bfloat16)
    stay = lambda a: pltpu.with_memory_space_constraint(a, pltpu.HBM)
    tokens, weights = stay(tokens), stay(w_qkv.transpose(1, 0, 2))
    offset_mid, offset_far, w_out = stay(offset_mid), stay(offset_far), stay(w_out)
    deep = 512

    groups = segments(seq_count)
    across = [[g[2 * i + c] for i in range(SPAN // 2)] for g in groups for c in range(2)]
    chips = [list(range(c, seq_count, 2)) for c in range(2)]
    cores = [(i, i ^ 1) for i in range(seq_count)]
    near_count, far_count = len(across[0]), len(chips[0])
    steps = width // deep
    tok_scratch = pltpu.VMEM((steps, rows, deep), jnp.bfloat16)

    off_scratch = [
        pltpu.SMEM((heads,), jnp.int32),
        pltpu.SMEM((heads,), jnp.int32),
        pltpu.SemaphoreType.DMA((2,)),
    ]

    kv, mid_kv, far_kv = pl.pallas_call(
        functools.partial(kv_kernel, *sizes),
        in_specs=[HBM] * 4,
        out_specs=[VMEM] * 3,
        out_shape=[
            bf16(2, rows, cols),
            bf16(1, 2, heads, mid_rows, size),
            bf16(far_count, 2, 4 * heads, size),
        ],
        scratch_shapes=[
            tok_scratch,
            pltpu.VMEM((2, steps, deep, cols), jnp.bfloat16),
            pltpu.VMEM((4 * heads, size), jnp.float32),
            *off_scratch,
            pltpu.SemaphoreType.DMA((3 * steps,)),
        ],
        compiler_params=params(20),
        name="keys_values",
    )(offset_mid, offset_far, tokens, weights)

    far_line = lax.all_to_all(far_kv, "seq", 0, 0, axis_index_groups=chips)
    mid_pieces = share(mid_kv[0], "seq", across)
    own = rows // head_count
    place_arr = place.astype(jnp.int32).reshape(1)
    near, sel, own_tokens = pl.pallas_call(
        functools.partial(near_kernel, *sizes),
        in_specs=[HBM, HBM, SMEM, HBM, HBM, VMEM],
        out_specs=[VMEM] * 3,
        out_shape=[bf16(rows, cols), bf16(heads, PICKS, size), bf16(own, width)],
        scratch_shapes=[
            tok_scratch,
            pltpu.VMEM((1, steps, deep, cols), jnp.bfloat16),
            *off_scratch,
            pltpu.SemaphoreType.DMA((2 * steps,)),
        ],
        compiler_params=params(14),
        name="near",
    )(offset_mid, offset_far, place_arr, tokens, weights, kv)

    *mid_pieces, near = lax.optimization_barrier((*mid_pieces, near))
    mid_line = jnp.stack(mid_pieces)
    mid_other = lax.ppermute(mid_line, "seq", cores)
    far_other = lax.ppermute(far_line, "seq", cores)

    half = width // 2
    kept_a, sent_a, kept_b, sent_b = pl.pallas_call(
        functools.partial(wide_kernel, *sizes, head_count),
        in_specs=[HBM, HBM, SMEM] + [VMEM] * 7 + [HBM],
        out_specs=[VMEM] * 4,
        out_shape=[bf16(2 * own, half)] * 4,
        scratch_shapes=[
            pltpu.VMEM((rows, cols), jnp.float32),
            *off_scratch,
            pltpu.VMEM(w_out.shape, jnp.bfloat16),
            pltpu.SemaphoreType.DMA,
        ],
        compiler_params=params(14),
        name="wide",
    )(
        offset_mid, offset_far, place_arr, sel, kv, near,
        mid_line, mid_other, far_line, far_other, w_out,
    )

    swap = lambda a, step: lax.ppermute(a, "head", [(i, i ^ step) for i in range(head_count)])
    got_a, got_b = swap(sent_a, 1), swap(sent_b, 3)
    tail = lambda a: a[own:].astype(jnp.float32)
    last_a = swap((tail(kept_a) + tail(got_a)).astype(jnp.bfloat16), 3)
    last_b = swap((tail(kept_b) + tail(got_b)).astype(jnp.bfloat16), 1)
    got = [kept_a, got_a, last_a, kept_b, got_b, last_b]

    logit = pl.pallas_call(
        logits_kernel,
        in_specs=[VMEM] * (3 + len(got)),
        out_specs=VMEM,
        out_shape=jax.ShapeDtypeStruct((own, w_label.shape[1]), jnp.float32),
        compiler_params=params(10),
        name="logits",
    )(own_tokens, norm_gain.reshape(1, width), w_label, *got)

    every = share(logit, "head", [list(range(head_count))])
    logits = jnp.zeros((head_count,) + logit.shape, jnp.float32)
    for step in range(head_count):
        logits = lax.dynamic_update_index_in_dim(logits, every[step], place ^ step, 0)
    return logits.reshape(rows, -1)


def solution(mesh):
    return jax.shard_map(
        body,
        mesh=mesh,
        in_specs=(
            P("seq", None),
            P(None, None, "head"),
            P("head", None),
            P(),
            P(),
            P("head"),
            P("head"),
        ),
        out_specs=P("seq", None),
        check_vma=False,
    )
```
